256 devices in a mesh: gx: 16 (over y, x), gy: 16 (over z, core).
Axes of the slice: x: 4, y: 4, z: 8, core: 2. Of those that a mesh axis runs over, the one named last changes fastest.
Arguments:
- state: float32 [1024, 6, 16, 16, 128], P(('gx', 'gy')), may hold values from -1 to 4, as said below
- metrics: bfloat16 [1024, 10, 16, 16, 128], P(('gx', 'gy')), may hold values from -0.3 to 1.4, as said below
- nbr_block: int32 [1024, 4], P(('gx', 'gy')), may hold values from 0 to 1023, as said below
- nbr_face: int32 [1024, 4], P(('gx', 'gy')), may hold values from 0 to 3
- flip: int32 [1024, 4], P(('gx', 'gy')), may hold values from 0 to 1
- bc_code: int32 [1024, 4], P(('gx', 'gy')), may hold values from 0 to 3
Outputs:
- new_state: float32 [1024, 6, 16, 16, 128], P(('gx', 'gy'))
- residual: float32 [1024, 6, 16, 16, 128], P(('gx', 'gy'))
The draws below stay inside these ranges and needn't reach their ends.
Inputs may be any that keep to these rules, and one draw needn't show every extreme that they name: `nbr_block`: an interface face's neighbour block lies on the same device or on a device whose index differs by one along exactly one of gx and gy. Connectivity is mutual: if face f of block b meets face f2 of block b2, then face f2 of b2 meets face f of b with the same flip. Faces with bc_code other than 0 name their own block and face with flip 0. The faces of one device's blocks meet at most 4 faces of blocks of a device beside it along gy, and at most one face of blocks of a device beside it along gx; both bounds are reached. `state`: density and pressure are positive. `metrics`: volumes are positive.
All inputs are finite; a program needn't handle non-finite values.
Results may differ from the reference program's by a relative error of at most 0.0003.
Values sent between devices are 32-bit elements; how exact they have to be, the bound alone decides.
A program may use at most 64 MiB of HBM per device.

```python
import jax
import jax.numpy as jnp
import numpy as np
from jax import lax

C = 16
K = 128
NB = 4
NBLK = 1024
N_GX = 16
N_GY = 16


TABLE_LOGICAL = np.array([[0, 1, 2, 3], [2, 3, 1, 0], [1, 0, 3, 2], [3, 2, 0, 1]], np.int32)


TABLE_SIGN = np.array([[1, 1, 1, 1], [-1, -1, 1, 1], [-1, -1, -1, -1], [1, 1, -1, -1]], np.int32)


TABLE_INVERSE = np.array([[0, 1, 2, 3], [3, 2, 0, 1], [1, 0, 3, 2], [2, 3, 1, 0]], np.int32)


OPPOSITE = np.array([1, 0, 3, 2], np.int32)


STEP_COLUMN = np.array([-1, 1, 0, 0], np.int32)


STEP_ROW = np.array([0, 0, -1, 1], np.int32)


BOUNDARY = np.array([2, 3, 1, 2], np.int32)


def layout(key):
    key_row = jax.random.fold_in(key, 12)
    key_rot = jax.random.fold_in(key, 13)
    count = N_GX * N_GY
    height = N_GX * NB
    rows = jax.vmap(lambda sub: jax.random.permutation(sub, NB))(jax.random.split(key_row, count)).astype(jnp.int32)
    rotation = jax.random.randint(key_rot, (NBLK,), 0, 4)
    owned = jnp.arange(count, dtype=jnp.int32)[:, None] * NB + rows
    grid = owned.reshape(N_GX, N_GY, NB).transpose(0, 2, 1).reshape(height, N_GY)
    table_logical = jnp.array(TABLE_LOGICAL)
    table_sign = jnp.array(TABLE_SIGN)
    table_inverse = jnp.array(TABLE_INVERSE)
    rot = rotation[grid]
    logical = table_logical[rot]
    sign = table_sign[rot]
    col_index = jnp.arange(N_GY, dtype=jnp.int32)[None, :, None] + jnp.array(STEP_COLUMN)[logical]
    row_index = jnp.arange(height, dtype=jnp.int32)[:, None, None] + jnp.array(STEP_ROW)[logical]
    inside = (col_index >= 0) & (col_index < N_GY) & (row_index >= 0) & (row_index < height)
    neighbour = grid[jnp.clip(row_index, 0, height - 1), jnp.clip(col_index, 0, N_GY - 1)]
    near_rot = rotation[neighbour]
    near_face = table_inverse[near_rot, jnp.array(OPPOSITE)[logical]]
    near_sign = table_sign[near_rot, near_face]
    own_face = jnp.broadcast_to(jnp.arange(4, dtype=jnp.int32), logical.shape)
    own_block = jnp.broadcast_to(grid[..., None], logical.shape)
    code = jnp.where(inside, 0, jnp.array(BOUNDARY)[logical])
    block_out = jnp.where(inside, neighbour, own_block)
    face_out = jnp.where(inside, near_face, own_face)
    flip_out = jnp.where(inside & (sign != near_sign), 1, 0)
    flat = grid.reshape(-1)

    def place(values):
        return jnp.zeros((NBLK, 4), jnp.int32).at[flat].set(values.reshape(-1, 4).astype(jnp.int32))
    return (place(block_out), place(face_out), place(flip_out), place(code))


def draw_nbr_block(key, part):
    return layout(key)[0]


def draw_nbr_face(key, part):
    return layout(key)[1]


def draw_flip(key, part):
    return layout(key)[2]


def draw_bc_code(key, part):
    return layout(key)[3]


def draw_state(key, part):
    keys = jax.random.split(jax.random.fold_in(key, 21), 4)
    shape = (NBLK, C, C, K)
    density = jax.random.uniform(keys[0], shape, jnp.float32, 0.7, 1.3)
    velocity = jax.random.uniform(keys[1], (3,) + shape, jnp.float32, -0.3, 0.3)
    pressure = jax.random.uniform(keys[2], shape, jnp.float32, 0.6, 1.0)
    eddy = jax.random.uniform(keys[3], shape, jnp.float32, 0.02, 0.2)
    energy = pressure / 0.4 + 0.5 * density * jnp.sum(velocity * velocity, axis=0)
    return jnp.stack([density, density * velocity[0], density * velocity[1], density * velocity[2], energy, density * eddy], 1)


def draw_metrics(key, part):
    keys = jax.random.split(jax.random.fold_in(key, 31), 3)
    shape = (NBLK, C, C, K)
    side = jax.random.uniform(keys[0], (NBLK, 9, C, C, K), jnp.float32, -0.2, 0.2)
    main = jax.random.uniform(keys[1], (NBLK, 9, C, C, K), jnp.float32, 0.7, 1.3)
    diagonal = (jnp.arange(9) % 4 == 0)[None, :, None, None, None]
    vectors = jnp.where(diagonal, main, side)
    volume = jax.random.uniform(keys[2], shape, jnp.float32, 0.7, 1.3)
    return jnp.concatenate([vectors, volume[:, None]], 1).astype(jnp.bfloat16)


def setup_inputs(seed: int = 0) -> dict:
    streams_of = jax.random.split(jax.random.key(seed), 7)
    state = draw_state(jax.random.fold_in(streams_of[6], 71), 0)
    metrics = draw_metrics(jax.random.fold_in(streams_of[6], 71), 0)
    nbr_block = draw_nbr_block(jax.random.fold_in(streams_of[6], 71), 0)
    nbr_face = draw_nbr_face(jax.random.fold_in(streams_of[6], 71), 0)
    flip = draw_flip(jax.random.fold_in(streams_of[6], 71), 0)
    bc_code = draw_bc_code(jax.random.fold_in(streams_of[6], 71), 0)
    return {"state": state, "metrics": metrics, "nbr_block": nbr_block, "nbr_face": nbr_face, "flip": flip, "bc_code": bc_code}


GAMMA = 1.4
GAMMA_MINUS = 0.4
VISCOSITY = 0.02
CFL_NUMBER = 0.5
CB_ONE = 0.1355
CW_ONE = 3.24

def wall_sign():
    return jnp.array([1.0, -1.0, -1.0, -1.0, 1.0, -1.0], jnp.float32)

def free_stream():
    return jnp.array([1.0, 0.5, 0.0, 0.1, 2.1325, 0.05], jnp.float32)

def euler_flux(cons, area):
    density = cons[0]
    velocity = cons[1:4] / density
    pressure = GAMMA_MINUS * (cons[4] - 0.5 * lax.optimization_barrier(jnp.sum(cons[1:4] * velocity, axis=0)))
    normal = lax.optimization_barrier(jnp.sum(velocity * area, axis=0))
    sound = jnp.sqrt(GAMMA * jnp.abs(pressure) / density)
    flux = jnp.concatenate([cons[0:1] * normal, cons[1:4] * normal + pressure * area, ((cons[4] + pressure) * normal)[None], (cons[5] * normal)[None]], 0)
    speed = jnp.abs(normal) + sound * jnp.sqrt(lax.optimization_barrier(jnp.sum(area * area, axis=0)))
    return (flux, speed)

def face_average(values, axis):
    count = values.shape[axis]
    padded = jnp.concatenate([lax.slice_in_dim(values, 0, 1, axis=axis), values, lax.slice_in_dim(values, count - 1, count, axis=axis)], axis)
    return 0.5 * (lax.slice_in_dim(padded, 0, count + 1, axis=axis) + lax.slice_in_dim(padded, 1, count + 2, axis=axis))

def flux_balance(padded, normals, volume, axis):
    count = normals.shape[axis]
    area = face_average(normals, axis)
    face_volume = face_average(volume, axis - 1)
    left = lax.slice_in_dim(padded, 0, count + 1, axis=axis)
    right = lax.slice_in_dim(padded, 1, count + 2, axis=axis)
    flux_left, speed_left = euler_flux(left, area)
    flux_right, speed_right = euler_flux(right, area)
    jump = right - left
    flux = 0.5 * (flux_left + flux_right) - 0.5 * jnp.maximum(speed_left, speed_right) * jump
    eddy = 0.5 * (left[5] / left[0] + right[5] / right[0])
    coeff = (VISCOSITY + eddy) * lax.optimization_barrier(jnp.sum(area * area, axis=0)) / face_volume
    viscous = jnp.concatenate([jnp.zeros_like(jump[0:1]), coeff * jump[1:]], 0)
    flux = flux - viscous
    return lax.slice_in_dim(flux, 1, count + 1, axis=axis) - lax.slice_in_dim(flux, 0, count, axis=axis)

def velocity_change(padded, axis):
    count = padded.shape[axis] - 2
    velocity = padded[1:4] / padded[0]
    return 0.5 * (lax.slice_in_dim(velocity, 2, count + 2, axis=axis) - lax.slice_in_dim(velocity, 0, count, axis=axis))

def block_residual(cells, halos, metric):
    length = cells.shape[3]
    geometry = metric.astype(jnp.float32)
    normal_i, normal_j, normal_k, volume = (geometry[0:3], geometry[3:6], geometry[6:9], geometry[9])
    along_i = jnp.concatenate([halos[0][:, None], cells, halos[1][:, None]], 1)
    along_j = jnp.concatenate([halos[2][:, :, None], cells, halos[3][:, :, None]], 2)
    wall = cells[:, :, :, 0:1] * wall_sign()[:, None, None, None]
    freely = jnp.broadcast_to(free_stream()[:, None, None, None], wall.shape)
    along_k = jnp.concatenate([wall, cells, freely], 3)
    balance = flux_balance(along_i, normal_i, volume, 1) + flux_balance(along_j, normal_j, volume, 2) + flux_balance(along_k, normal_k, volume, 3)
    tensor = (velocity_change(along_i, 1)[:, None] * normal_i[None] + velocity_change(along_j, 2)[:, None] * normal_j[None] + velocity_change(along_k, 3)[:, None] * normal_k[None]) / volume
    vorticity = jnp.stack([tensor[2, 1] - tensor[1, 2], tensor[0, 2] - tensor[2, 0], tensor[1, 0] - tensor[0, 1]], 0)
    omega = jnp.sqrt(lax.optimization_barrier(jnp.sum(vorticity * vorticity, axis=0)) + 0.0001)
    eddy = cells[5] / cells[0]
    distance = 1.0 + 4.0 * jnp.arange(length, dtype=jnp.float32) / length
    source = CB_ONE * omega * cells[5] - CW_ONE * cells[5] * eddy / (distance * distance)
    residual = balance / volume
    return jnp.concatenate([residual[0:5], (residual[5] - source)[None]], 0)

def time_limit(cells, metric):
    geometry = metric.astype(jnp.float32)
    total = euler_flux(cells, geometry[0:3])[1] + euler_flux(cells, geometry[3:6])[1] + euler_flux(cells, geometry[6:9])[1]
    return jnp.min(geometry[9] / total)

def face_layers(cells):
    return jnp.stack([cells[:, 0], cells[:, -1], cells[:, :, 0], cells[:, :, -1]], 0)

def boundary_halo(fetched, own, flip, bc_code):
    turned = jnp.where(flip[..., None, None, None] == 1, jnp.flip(fetched, -2), fetched)
    wall = own * wall_sign()[:, None, None]
    freely = jnp.broadcast_to(free_stream()[:, None, None], own.shape)
    code = bc_code[..., None, None, None]
    return jnp.where(code == 0, turned, jnp.where(code == 1, wall, jnp.where(code == 2, freely, own)))

def residual_all(state, metrics, nbr_block, nbr_face, flip, bc_code):
    layers = jax.vmap(face_layers)(state)
    fetched = layers[nbr_block, nbr_face]
    halos = boundary_halo(fetched, layers, flip, bc_code)
    return lax.map(lambda operands: block_residual(operands[0], operands[1], operands[2]), (state, halos, metrics))

def reference(state, metrics, nbr_block, nbr_face, flip, bc_code):
    limits = lax.map(lambda operands: time_limit(operands[0], operands[1]), (state, metrics))
    step = CFL_NUMBER * jnp.min(limits)
    first = residual_all(state, metrics, nbr_block, nbr_face, flip, bc_code)
    middle = state - 0.5 * step * first
    second = residual_all(middle, metrics, nbr_block, nbr_face, flip, bc_code)
    return (state - step * second, second)
```

```python
import jax
import jax.numpy as jnp
from jax import lax
from jax.sharding import PartitionSpec as P

GAMMA = 1.4
GAMMA_MINUS = 0.4
VISCOSITY = 0.02
CFL_NUMBER = 0.5
CB_ONE = 0.1355
CW_ONE = 3.24


def shifted(value, axis, steps):
    count = lax.axis_size(axis)
    initial, last = (max(0, -steps), min(count, count - steps))
    return lax.ppermute(value, axis, [(source, source + steps) for source in range(initial, last)])


def wall_sign():
    return jnp.array([1.0, -1.0, -1.0, -1.0, 1.0, -1.0], jnp.float32)


def free_stream():
    return jnp.array([1.0, 0.5, 0.0, 0.1, 2.1325, 0.05], jnp.float32)


def euler_flux(cons, area):
    density = cons[0]
    velocity = cons[1:4] / density
    pressure = GAMMA_MINUS * (cons[4] - 0.5 * jnp.sum(cons[1:4] * velocity, axis=0))
    normal = jnp.sum(velocity * area, axis=0)
    sound = jnp.sqrt(GAMMA * jnp.abs(pressure) / density)
    flux = jnp.concatenate(
        [
            cons[0:1] * normal,
            cons[1:4] * normal + pressure * area,
            ((cons[4] + pressure) * normal)[None],
            (cons[5] * normal)[None],
        ],
        0,
    )
    speed = jnp.abs(normal) + sound * jnp.sqrt(jnp.sum(area * area, axis=0))
    return (flux, speed)


def face_average(values, axis):
    count = values.shape[axis]
    padded = jnp.concatenate(
        [
            lax.slice_in_dim(values, 0, 1, axis=axis),
            values,
            lax.slice_in_dim(values, count - 1, count, axis=axis),
        ],
        axis,
    )
    return 0.5 * (
        lax.slice_in_dim(padded, 0, count + 1, axis=axis)
        + lax.slice_in_dim(padded, 1, count + 2, axis=axis)
    )


def flux_balance(padded, normals, volume, axis):
    count = normals.shape[axis]
    area = face_average(normals, axis)
    face_volume = face_average(volume, axis - 1)
    left = lax.slice_in_dim(padded, 0, count + 1, axis=axis)
    right = lax.slice_in_dim(padded, 1, count + 2, axis=axis)
    flux_left, speed_left = euler_flux(left, area)
    flux_right, speed_right = euler_flux(right, area)
    jump = right - left
    flux = 0.5 * (flux_left + flux_right) - 0.5 * jnp.maximum(speed_left, speed_right) * jump
    eddy = 0.5 * (left[5] / left[0] + right[5] / right[0])
    coeff = (VISCOSITY + eddy) * jnp.sum(area * area, axis=0) / face_volume
    viscous = jnp.concatenate([jnp.zeros_like(jump[0:1]), coeff * jump[1:]], 0)
    flux = flux - viscous
    return lax.slice_in_dim(flux, 1, count + 1, axis=axis) - lax.slice_in_dim(
        flux, 0, count, axis=axis
    )


def velocity_change(padded, axis):
    count = padded.shape[axis] - 2
    velocity = padded[1:4] / padded[0]
    return 0.5 * (
        lax.slice_in_dim(velocity, 2, count + 2, axis=axis)
        - lax.slice_in_dim(velocity, 0, count, axis=axis)
    )


def block_residual(cells, halos, metric):
    length = cells.shape[3]
    geometry = metric.astype(jnp.float32)
    normal_i, normal_j, normal_k, volume = (
        geometry[0:3],
        geometry[3:6],
        geometry[6:9],
        geometry[9],
    )
    along_i = jnp.concatenate([halos[0][:, None], cells, halos[1][:, None]], 1)
    along_j = jnp.concatenate([halos[2][:, :, None], cells, halos[3][:, :, None]], 2)
    wall = cells[:, :, :, 0:1] * wall_sign()[:, None, None, None]
    freely = jnp.broadcast_to(free_stream()[:, None, None, None], wall.shape)
    along_k = jnp.concatenate([wall, cells, freely], 3)
    balance = (
        flux_balance(along_i, normal_i, volume, 1)
        + flux_balance(along_j, normal_j, volume, 2)
        + flux_balance(along_k, normal_k, volume, 3)
    )
    tensor = (
        velocity_change(along_i, 1)[:, None] * normal_i[None]
        + velocity_change(along_j, 2)[:, None] * normal_j[None]
        + velocity_change(along_k, 3)[:, None] * normal_k[None]
    ) / volume
    vorticity = jnp.stack(
        [tensor[2, 1] - tensor[1, 2], tensor[0, 2] - tensor[2, 0], tensor[1, 0] - tensor[0, 1]], 0
    )
    omega = jnp.sqrt(jnp.sum(vorticity * vorticity, axis=0) + 0.0001)
    eddy = cells[5] / cells[0]
    distance = 1.0 + 4.0 * jnp.arange(length, dtype=jnp.float32) / length
    source = CB_ONE * omega * cells[5] - CW_ONE * cells[5] * eddy / (distance * distance)
    residual = balance / volume
    return jnp.concatenate([residual[0:5], (residual[5] - source)[None]], 0)


def time_limit(cells, metric):
    geometry = metric.astype(jnp.float32)
    total = (
        euler_flux(cells, geometry[0:3])[1]
        + euler_flux(cells, geometry[3:6])[1]
        + euler_flux(cells, geometry[6:9])[1]
    )
    return jnp.min(geometry[9] / total)


def face_layers(cells):
    return jnp.stack([cells[:, 0], cells[:, -1], cells[:, :, 0], cells[:, :, -1]], 0)


def boundary_halo(fetched, own, flip, bc_code):
    turned = jnp.where(flip[..., None, None, None] == 1, jnp.flip(fetched, -2), fetched)
    wall = own * wall_sign()[:, None, None]
    freely = jnp.broadcast_to(free_stream()[:, None, None], own.shape)
    code = bc_code[..., None, None, None]
    return jnp.where(
        code == 0, turned, jnp.where(code == 1, wall, jnp.where(code == 2, freely, own))
    )


def slot_of(marked, keys):
    same = marked[:, None] & marked[None, :]
    return jnp.sum(same & (keys[None, :] < keys[:, None]), axis=1)


def per_device(state, metrics, nbr_block, nbr_face, flip, bc_code):
    blocks = state.shape[0]
    groups = lax.axis_size("gy")
    grid_col = lax.axis_index("gy")
    grid_row = lax.axis_index("gx")
    partner = nbr_block.reshape(-1)
    facing = nbr_face.reshape(-1)
    interface = bc_code.reshape(-1) == 0
    far_device = partner // blocks
    far_row = far_device // groups
    far_col = far_device % groups
    own_key = jnp.arange(partner.shape[0], dtype=jnp.int32)
    far_key = partner % blocks * 4 + facing

    def toward(step_row, step_col):
        return interface & (far_row == grid_row + step_row) & (far_col == grid_col + step_col)

    def plan(step_row, step_col):
        sending = toward(step_row, step_col)
        taking = toward(-step_row, -step_col)
        return (sending, slot_of(sending, own_key), taking, slot_of(taking, far_key))

    row_plans = [plan(1, 0), plan(-1, 0)]
    col_plans = [plan(0, 1), plan(0, -1)]

    def pack(flat, sending, send_slot, capacity):
        outgoing = jnp.zeros((capacity,) + flat.shape[1:], jnp.float32)
        return outgoing.at[jnp.where(sending, send_slot, capacity)].set(flat, mode="drop")

    def halos_for(cells):
        layers = jax.vmap(face_layers)(cells)
        flat = layers.reshape((blocks * 4,) + layers.shape[2:])
        fetched = flat[far_key]
        for offset, entry in zip((1, -1), row_plans):
            outgoing = pack(flat, entry[0], entry[1], 1)
            incoming = shifted(outgoing, "gx", offset)
            fetched = jnp.where(
                entry[2][:, None, None, None], incoming[jnp.minimum(entry[3], 0)], fetched
            )
        for offset, entry in zip((1, -1), col_plans):
            outgoing = pack(flat, entry[0], entry[1], blocks)
            incoming = shifted(outgoing, "gy", offset)
            fetched = jnp.where(
                entry[2][:, None, None, None], incoming[jnp.minimum(entry[3], blocks - 1)], fetched
            )
        fetched = fetched.reshape(layers.shape)
        return boundary_halo(fetched, layers, flip, bc_code)

    def residual_local(cells):
        halos = halos_for(cells)
        return lax.map(
            lambda operands: block_residual(operands[0], operands[1], operands[2]),
            (cells, halos, metrics),
        )

    limits = lax.map(lambda operands: time_limit(operands[0], operands[1]), (state, metrics))
    step = CFL_NUMBER * lax.pmin(lax.pmin(jnp.min(limits), "gy"), "gx")
    first = residual_local(state)
    middle = state - 0.5 * step * first
    second = residual_local(middle)
    return (state - step * second, second)


def solution(mesh):
    return jax.shard_map(
        per_device,
        mesh=mesh,
        in_specs=(
            P(("gx", "gy"), None, None, None, None),
            P(("gx", "gy"), None, None, None, None),
            P(("gx", "gy"), None),
            P(("gx", "gy"), None),
            P(("gx", "gy"), None),
            P(("gx", "gy"), None),
        ),
        out_specs=(
            P(("gx", "gy"), None, None, None, None),
            P(("gx", "gy"), None, None, None, None),
        ),
        check_vma=False,
    )
```

```python
import jax
import jax.numpy as jnp
from jax import lax
from jax.sharding import PartitionSpec as P

GAMMA = 1.4
GAMMA_MINUS = 0.4
VISCOSITY = 0.02
CFL_NUMBER = 0.5
CB_ONE = 0.1355
CW_ONE = 3.24


def shifted(value, axis, steps):
    count = lax.axis_size(axis)
    initial, last = (max(0, -steps), min(count, count - steps))
    return lax.ppermute(value, axis, [(source, source + steps) for source in range(initial, last)])


def wall_sign():
    return jnp.array([1.0, -1.0, -1.0, -1.0, 1.0, -1.0], jnp.float32)


def free_stream():
    return jnp.array([1.0, 0.5, 0.0, 0.1, 2.1325, 0.05], jnp.float32)


def euler_flux(cons, area):
    density = cons[0]
    velocity = cons[1:4] / density
    pressure = GAMMA_MINUS * (cons[4] - 0.5 * jnp.sum(cons[1:4] * velocity, axis=0))
    normal = jnp.sum(velocity * area, axis=0)
    sound = jnp.sqrt(GAMMA * jnp.abs(pressure) / density)
    flux = jnp.concatenate(
        [
            cons[0:1] * normal,
            cons[1:4] * normal + pressure * area,
            ((cons[4] + pressure) * normal)[None],
            (cons[5] * normal)[None],
        ],
        0,
    )
    speed = jnp.abs(normal) + sound * jnp.sqrt(jnp.sum(area * area, axis=0))
    return (flux, speed)


def face_average(values, axis):
    count = values.shape[axis]
    padded = jnp.concatenate(
        [
            lax.slice_in_dim(values, 0, 1, axis=axis),
            values,
            lax.slice_in_dim(values, count - 1, count, axis=axis),
        ],
        axis,
    )
    return 0.5 * (
        lax.slice_in_dim(padded, 0, count + 1, axis=axis)
        + lax.slice_in_dim(padded, 1, count + 2, axis=axis)
    )


def flux_balance(padded, normals, volume, axis):
    count = normals.shape[axis]
    area = face_average(normals, axis)
    face_volume = face_average(volume, axis - 1)
    left = lax.slice_in_dim(padded, 0, count + 1, axis=axis)
    right = lax.slice_in_dim(padded, 1, count + 2, axis=axis)
    flux_left, speed_left = euler_flux(left, area)
    flux_right, speed_right = euler_flux(right, area)
    jump = right - left
    flux = 0.5 * (flux_left + flux_right) - 0.5 * jnp.maximum(speed_left, speed_right) * jump
    eddy = 0.5 * (left[5] / left[0] + right[5] / right[0])
    coeff = (VISCOSITY + eddy) * jnp.sum(area * area, axis=0) / face_volume
    viscous = jnp.concatenate([jnp.zeros_like(jump[0:1]), coeff * jump[1:]], 0)
    flux = flux - viscous
    return lax.slice_in_dim(flux, 1, count + 1, axis=axis) - lax.slice_in_dim(
        flux, 0, count, axis=axis
    )


def velocity_change(padded, axis):
    count = padded.shape[axis] - 2
    velocity = padded[1:4] / padded[0]
    return 0.5 * (
        lax.slice_in_dim(velocity, 2, count + 2, axis=axis)
        - lax.slice_in_dim(velocity, 0, count, axis=axis)
    )


def block_residual(cells, halos, metric):
    length = cells.shape[3]
    geometry = metric.astype(jnp.float32)
    normal_i, normal_j, normal_k, volume = (
        geometry[0:3],
        geometry[3:6],
        geometry[6:9],
        geometry[9],
    )
    along_i = jnp.concatenate([halos[0][:, None], cells, halos[1][:, None]], 1)
    along_j = jnp.concatenate([halos[2][:, :, None], cells, halos[3][:, :, None]], 2)
    wall = cells[:, :, :, 0:1] * wall_sign()[:, None, None, None]
    freely = jnp.broadcast_to(free_stream()[:, None, None, None], wall.shape)
    along_k = jnp.concatenate([wall, cells, freely], 3)
    balance = (
        flux_balance(along_i, normal_i, volume, 1)
        + flux_balance(along_j, normal_j, volume, 2)
        + flux_balance(along_k, normal_k, volume, 3)
    )
    tensor = (
        velocity_change(along_i, 1)[:, None] * normal_i[None]
        + velocity_change(along_j, 2)[:, None] * normal_j[None]
        + velocity_change(along_k, 3)[:, None] * normal_k[None]
    ) / volume
    vorticity = jnp.stack(
        [tensor[2, 1] - tensor[1, 2], tensor[0, 2] - tensor[2, 0], tensor[1, 0] - tensor[0, 1]], 0
    )
    omega = jnp.sqrt(jnp.sum(vorticity * vorticity, axis=0) + 0.0001)
    eddy = cells[5] / cells[0]
    distance = 1.0 + 4.0 * jnp.arange(length, dtype=jnp.float32) / length
    source = CB_ONE * omega * cells[5] - CW_ONE * cells[5] * eddy / (distance * distance)
    residual = balance / volume
    return jnp.concatenate([residual[0:5], (residual[5] - source)[None]], 0)


def time_limit(cells, metric):
    geometry = metric.astype(jnp.float32)
    total = (
        euler_flux(cells, geometry[0:3])[1]
        + euler_flux(cells, geometry[3:6])[1]
        + euler_flux(cells, geometry[6:9])[1]
    )
    return jnp.min(geometry[9] / total)


def face_layers(cells):
    return jnp.stack([cells[:, 0], cells[:, -1], cells[:, :, 0], cells[:, :, -1]], 0)


def boundary_halo(fetched, own, flip, bc_code):
    turned = jnp.where(flip[..., None, None, None] == 1, jnp.flip(fetched, -2), fetched)
    wall = own * wall_sign()[:, None, None]
    freely = jnp.broadcast_to(free_stream()[:, None, None], own.shape)
    code = bc_code[..., None, None, None]
    return jnp.where(
        code == 0, turned, jnp.where(code == 1, wall, jnp.where(code == 2, freely, own))
    )


def slot_of(marked, keys):
    same = marked[:, None] & marked[None, :]
    return jnp.sum(same & (keys[None, :] < keys[:, None]), axis=1)


def per_device(state, metrics, nbr_block, nbr_face, flip, bc_code):
    blocks = state.shape[0]
    groups = lax.axis_size("gy")
    grid_col = lax.axis_index("gy")
    grid_row = lax.axis_index("gx")
    partner = nbr_block.reshape(-1)
    facing = nbr_face.reshape(-1)
    interface = bc_code.reshape(-1) == 0
    far_device = partner // blocks
    far_row = far_device // groups
    far_col = far_device % groups
    own_key = jnp.arange(partner.shape[0], dtype=jnp.int32)
    far_key = partner % blocks * 4 + facing

    def toward(step_row, step_col):
        return interface & (far_row == grid_row + step_row) & (far_col == grid_col + step_col)

    def plan(step_row, step_col):
        sending = toward(step_row, step_col)
        taking = toward(-step_row, -step_col)
        return (sending, slot_of(sending, own_key), taking, slot_of(taking, far_key))

    row_plans = [plan(1, 0), plan(-1, 0)]
    col_plans = [plan(0, 1), plan(0, -1)]

    def pack(flat, sending, send_slot, capacity):
        outgoing = jnp.zeros((capacity,) + flat.shape[1:], jnp.float32)
        return outgoing.at[jnp.where(sending, send_slot, capacity)].set(flat, mode="drop")

    def halos_for(cells):
        layers = jax.vmap(face_layers)(cells)
        flat = layers.reshape((blocks * 4,) + layers.shape[2:])
        fetched = flat[far_key]
        for offset, entry in zip((1, -1), row_plans):
            outgoing = pack(flat, entry[0], entry[1], 1)
            incoming = shifted(outgoing, "gx", offset)
            fetched = jnp.where(
                entry[2][:, None, None, None], incoming[jnp.minimum(entry[3], 0)], fetched
            )
        for offset, entry in zip((1, -1), col_plans):
            outgoing = pack(flat, entry[0], entry[1], blocks)
            incoming = shifted(outgoing, "gy", offset)
            fetched = jnp.where(
                entry[2][:, None, None, None], incoming[jnp.minimum(entry[3], blocks - 1)], fetched
            )
        fetched = fetched.reshape(layers.shape)
        return boundary_halo(fetched, layers, flip, bc_code)

    def residual_local(cells):
        halos = halos_for(cells)
        return lax.map(
            lambda operands: block_residual(operands[0], operands[1], operands[2]),
            (cells, halos, metrics),
        )

    limits = lax.map(lambda operands: time_limit(operands[0], operands[1]), (state, metrics))
    gathered = lax.all_gather(jnp.broadcast_to(jnp.min(limits), (1024,)), ("gx", "gy"), tiled=True)
    step = CFL_NUMBER * jnp.min(gathered)
    first = residual_local(state)
    middle = state - 0.5 * step * first
    second = residual_local(middle)
    return (state - step * second, second)


def solution(mesh):
    return jax.shard_map(
        per_device,
        mesh=mesh,
        in_specs=(
            P(("gx", "gy"), None, None, None, None),
            P(("gx", "gy"), None, None, None, None),
            P(("gx", "gy"), None),
            P(("gx", "gy"), None),
            P(("gx", "gy"), None),
            P(("gx", "gy"), None),
        ),
        out_specs=(
            P(("gx", "gy"), None, None, None, None),
            P(("gx", "gy"), None, None, None, None),
        ),
        check_vma=False,
    )
```

```python
import jax
import jax.numpy as jnp
from jax import lax
from jax.sharding import PartitionSpec as P

GAMMA = 1.4
GAMMA_MINUS = 0.4
VISCOSITY = 0.02
CFL_NUMBER = 0.5
CB_ONE = 0.1355
CW_ONE = 3.24


def shifted(value, axis, steps):
    count = lax.axis_size(axis)
    initial, last = (max(0, -steps), min(count, count - steps))
    return lax.ppermute(value, axis, [(source, source + steps) for source in range(initial, last)])


def wall_sign():
    return jnp.array([1.0, -1.0, -1.0, -1.0, 1.0, -1.0], jnp.float32)


def free_stream():
    return jnp.array([1.0, 0.5, 0.0, 0.1, 2.1325, 0.05], jnp.float32)


def euler_flux(cons, area):
    density = cons[0]
    velocity = cons[1:4] / density
    pressure = GAMMA_MINUS * (cons[4] - 0.5 * jnp.sum(cons[1:4] * velocity, axis=0))
    normal = jnp.sum(velocity * area, axis=0)
    sound = jnp.sqrt(GAMMA * jnp.abs(pressure) / density)
    flux = jnp.concatenate(
        [
            cons[0:1] * normal,
            cons[1:4] * normal + pressure * area,
            ((cons[4] + pressure) * normal)[None],
            (cons[5] * normal)[None],
        ],
        0,
    )
    speed = jnp.abs(normal) + sound * jnp.sqrt(jnp.sum(area * area, axis=0))
    return (flux, speed)


def face_average(values, axis):
    count = values.shape[axis]
    padded = jnp.concatenate(
        [
            lax.slice_in_dim(values, 0, 1, axis=axis),
            values,
            lax.slice_in_dim(values, count - 1, count, axis=axis),
        ],
        axis,
    )
    return 0.5 * (
        lax.slice_in_dim(padded, 0, count + 1, axis=axis)
        + lax.slice_in_dim(padded, 1, count + 2, axis=axis)
    )


def flux_balance(padded, normals, volume, axis):
    count = normals.shape[axis]
    area = face_average(normals, axis)
    face_volume = face_average(volume, axis - 1)
    left = lax.slice_in_dim(padded, 0, count + 1, axis=axis)
    right = lax.slice_in_dim(padded, 1, count + 2, axis=axis)
    flux_left, speed_left = euler_flux(left, area)
    flux_right, speed_right = euler_flux(right, area)
    jump = right - left
    flux = 0.5 * (flux_left + flux_right) - 0.5 * jnp.maximum(speed_left, speed_right) * jump
    eddy = 0.5 * (left[5] / left[0] + right[5] / right[0])
    coeff = (VISCOSITY + eddy) * jnp.sum(area * area, axis=0) / face_volume
    viscous = jnp.concatenate([jnp.zeros_like(jump[0:1]), coeff * jump[1:]], 0)
    flux = flux - viscous
    return lax.slice_in_dim(flux, 1, count + 1, axis=axis) - lax.slice_in_dim(
        flux, 0, count, axis=axis
    )


def velocity_change(padded, axis):
    count = padded.shape[axis] - 2
    velocity = padded[1:4] / padded[0]
    return 0.5 * (
        lax.slice_in_dim(velocity, 2, count + 2, axis=axis)
        - lax.slice_in_dim(velocity, 0, count, axis=axis)
    )


def block_residual(cells, halos, metric):
    length = cells.shape[3]
    geometry = metric.astype(jnp.float32)
    normal_i, normal_j, normal_k, volume = (
        geometry[0:3],
        geometry[3:6],
        geometry[6:9],
        geometry[9],
    )
    along_i = jnp.concatenate([halos[0][:, None], cells, halos[1][:, None]], 1)
    along_j = jnp.concatenate([halos[2][:, :, None], cells, halos[3][:, :, None]], 2)
    wall = cells[:, :, :, 0:1] * wall_sign()[:, None, None, None]
    freely = jnp.broadcast_to(free_stream()[:, None, None, None], wall.shape)
    along_k = jnp.concatenate([wall, cells, freely], 3)
    balance = (
        flux_balance(along_i, normal_i, volume, 1)
        + flux_balance(along_j, normal_j, volume, 2)
        + flux_balance(along_k, normal_k, volume, 3)
    )
    tensor = (
        velocity_change(along_i, 1)[:, None] * normal_i[None]
        + velocity_change(along_j, 2)[:, None] * normal_j[None]
        + velocity_change(along_k, 3)[:, None] * normal_k[None]
    ) / volume
    vorticity = jnp.stack(
        [tensor[2, 1] - tensor[1, 2], tensor[0, 2] - tensor[2, 0], tensor[1, 0] - tensor[0, 1]], 0
    )
    omega = jnp.sqrt(jnp.sum(vorticity * vorticity, axis=0) + 0.0001)
    eddy = cells[5] / cells[0]
    distance = 1.0 + 4.0 * jnp.arange(length, dtype=jnp.float32) / length
    source = CB_ONE * omega * cells[5] - CW_ONE * cells[5] * eddy / (distance * distance)
    residual = balance / volume
    return jnp.concatenate([residual[0:5], (residual[5] - source)[None]], 0)


def time_limit(cells, metric):
    geometry = metric.astype(jnp.float32)
    total = (
        euler_flux(cells, geometry[0:3])[1]
        + euler_flux(cells, geometry[3:6])[1]
        + euler_flux(cells, geometry[6:9])[1]
    )
    return jnp.min(geometry[9] / total)


def face_layers(cells):
    return jnp.stack([cells[:, 0], cells[:, -1], cells[:, :, 0], cells[:, :, -1]], 0)


def boundary_halo(fetched, own, flip, bc_code):
    turned = jnp.where(flip[..., None, None, None] == 1, jnp.flip(fetched, -2), fetched)
    wall = own * wall_sign()[:, None, None]
    freely = jnp.broadcast_to(free_stream()[:, None, None], own.shape)
    code = bc_code[..., None, None, None]
    return jnp.where(
        code == 0, turned, jnp.where(code == 1, wall, jnp.where(code == 2, freely, own))
    )


def slot_of(marked, keys):
    same = marked[:, None] & marked[None, :]
    return jnp.sum(same & (keys[None, :] < keys[:, None]), axis=1)


def per_device(state, metrics, nbr_block, nbr_face, flip, bc_code):
    blocks = state.shape[0]
    groups = lax.axis_size("gy")
    grid_col = lax.axis_index("gy")
    grid_row = lax.axis_index("gx")
    partner = nbr_block.reshape(-1)
    facing = nbr_face.reshape(-1)
    interface = bc_code.reshape(-1) == 0
    far_device = partner // blocks
    far_row = far_device // groups
    far_col = far_device % groups
    own_key = jnp.arange(partner.shape[0], dtype=jnp.int32)
    far_key = partner % blocks * 4 + facing

    def toward(step_row, step_col):
        return interface & (far_row == grid_row + step_row) & (far_col == grid_col + step_col)

    def plan(step_row, step_col):
        sending = toward(step_row, step_col)
        taking = toward(-step_row, -step_col)
        return (sending, slot_of(sending, own_key), taking, slot_of(taking, far_key))

    row_plans = [plan(1, 0), plan(-1, 0)]
    col_plans = [plan(0, 1), plan(0, -1)]

    def pack(flat, sending, send_slot, capacity):
        outgoing = jnp.zeros((capacity,) + flat.shape[1:], jnp.float32)
        return outgoing.at[jnp.where(sending, send_slot, capacity)].set(flat, mode="drop")

    def halos_for(cells):
        layers = jax.vmap(face_layers)(cells)
        flat = layers.reshape((blocks * 4,) + layers.shape[2:])
        fetched = flat[far_key]
        for offset, entry in zip((1, -1), row_plans):
            outgoing = pack(flat, entry[0], entry[1], 1)
            incoming = shifted(outgoing, "gx", offset)
            fetched = jnp.where(
                entry[2][:, None, None, None], incoming[jnp.minimum(entry[3], 0)], fetched
            )
        for offset, entry in zip((1, -1), col_plans):
            outgoing = pack(flat, entry[0], entry[1], blocks)
            incoming = shifted(outgoing, "gy", offset)
            fetched = jnp.where(
                entry[2][:, None, None, None], incoming[jnp.minimum(entry[3], blocks - 1)], fetched
            )
        fetched = fetched.reshape(layers.shape)
        return boundary_halo(fetched, layers, flip, bc_code)

    def residual_local(cells):
        halos = halos_for(cells)
        return lax.map(
            lambda operands: block_residual(operands[0], operands[1], operands[2]),
            (cells, halos, metrics),
        )

    limits = jax.vmap(time_limit)(state, metrics)
    gathered = lax.all_gather(jnp.broadcast_to(jnp.min(limits), (1024,)), ("gx", "gy"), tiled=True)
    step = CFL_NUMBER * jnp.min(gathered)
    first = residual_local(state)
    middle = state - 0.5 * step * first
    second = residual_local(middle)
    return (state - step * second, second)


def solution(mesh):
    return jax.shard_map(
        per_device,
        mesh=mesh,
        in_specs=(
            P(("gx", "gy"), None, None, None, None),
            P(("gx", "gy"), None, None, None, None),
            P(("gx", "gy"), None),
            P(("gx", "gy"), None),
            P(("gx", "gy"), None),
            P(("gx", "gy"), None),
        ),
        out_specs=(
            P(("gx", "gy"), None, None, None, None),
            P(("gx", "gy"), None, None, None, None),
        ),
        check_vma=False,
    )
```

```python
import jax
import jax.numpy as jnp
from jax import lax
from jax.sharding import PartitionSpec as P

GAMMA = 1.4
GAMMA_MINUS = 0.4
VISCOSITY = 0.02
CFL_NUMBER = 0.5
CB_ONE = 0.1355
CW_ONE = 3.24


def shifted(value, axis, steps):
    count = lax.axis_size(axis)
    initial, last = (max(0, -steps), min(count, count - steps))
    return lax.ppermute(value, axis, [(source, source + steps) for source in range(initial, last)])


def wall_sign():
    return jnp.array([1.0, -1.0, -1.0, -1.0, 1.0, -1.0], jnp.float32)


def free_stream():
    return jnp.array([1.0, 0.5, 0.0, 0.1, 2.1325, 0.05], jnp.float32)


def euler_flux(cons, area):
    density = cons[0]
    velocity = cons[1:4] / density
    pressure = GAMMA_MINUS * (cons[4] - 0.5 * jnp.sum(cons[1:4] * velocity, axis=0))
    normal = jnp.sum(velocity * area, axis=0)
    sound = jnp.sqrt(GAMMA * jnp.abs(pressure) / density)
    flux = jnp.concatenate(
        [
            cons[0:1] * normal,
            cons[1:4] * normal + pressure * area,
            ((cons[4] + pressure) * normal)[None],
            (cons[5] * normal)[None],
        ],
        0,
    )
    speed = jnp.abs(normal) + sound * jnp.sqrt(jnp.sum(area * area, axis=0))
    return (flux, speed)


def face_average(values, axis):
    count = values.shape[axis]
    padded = jnp.concatenate(
        [
            lax.slice_in_dim(values, 0, 1, axis=axis),
            values,
            lax.slice_in_dim(values, count - 1, count, axis=axis),
        ],
        axis,
    )
    return 0.5 * (
        lax.slice_in_dim(padded, 0, count + 1, axis=axis)
        + lax.slice_in_dim(padded, 1, count + 2, axis=axis)
    )


def flux_balance(padded, normals, volume, axis):
    count = normals.shape[axis]
    area = face_average(normals, axis)
    face_volume = face_average(volume, axis - 1)
    left = lax.slice_in_dim(padded, 0, count + 1, axis=axis)
    right = lax.slice_in_dim(padded, 1, count + 2, axis=axis)
    flux_left, speed_left = euler_flux(left, area)
    flux_right, speed_right = euler_flux(right, area)
    jump = right - left
    flux = 0.5 * (flux_left + flux_right) - 0.5 * jnp.maximum(speed_left, speed_right) * jump
    eddy = 0.5 * (left[5] / left[0] + right[5] / right[0])
    coeff = (VISCOSITY + eddy) * jnp.sum(area * area, axis=0) / face_volume
    viscous = jnp.concatenate([jnp.zeros_like(jump[0:1]), coeff * jump[1:]], 0)
    flux = flux - viscous
    return lax.slice_in_dim(flux, 1, count + 1, axis=axis) - lax.slice_in_dim(
        flux, 0, count, axis=axis
    )


def velocity_change(padded, axis):
    count = padded.shape[axis] - 2
    velocity = padded[1:4] / padded[0]
    return 0.5 * (
        lax.slice_in_dim(velocity, 2, count + 2, axis=axis)
        - lax.slice_in_dim(velocity, 0, count, axis=axis)
    )


def block_residual(cells, halos, metric):
    length = cells.shape[3]
    geometry = metric.astype(jnp.float32)
    normal_i, normal_j, normal_k, volume = (
        geometry[0:3],
        geometry[3:6],
        geometry[6:9],
        geometry[9],
    )
    along_i = jnp.concatenate([halos[0][:, None], cells, halos[1][:, None]], 1)
    along_j = jnp.concatenate([halos[2][:, :, None], cells, halos[3][:, :, None]], 2)
    wall = cells[:, :, :, 0:1] * wall_sign()[:, None, None, None]
    freely = jnp.broadcast_to(free_stream()[:, None, None, None], wall.shape)
    along_k = jnp.concatenate([wall, cells, freely], 3)
    balance = (
        flux_balance(along_i, normal_i, volume, 1)
        + flux_balance(along_j, normal_j, volume, 2)
        + flux_balance(along_k, normal_k, volume, 3)
    )
    tensor = (
        velocity_change(along_i, 1)[:, None] * normal_i[None]
        + velocity_change(along_j, 2)[:, None] * normal_j[None]
        + velocity_change(along_k, 3)[:, None] * normal_k[None]
    ) / volume
    vorticity = jnp.stack(
        [tensor[2, 1] - tensor[1, 2], tensor[0, 2] - tensor[2, 0], tensor[1, 0] - tensor[0, 1]], 0
    )
    omega = jnp.sqrt(jnp.sum(vorticity * vorticity, axis=0) + 0.0001)
    eddy = cells[5] / cells[0]
    distance = 1.0 + 4.0 * jnp.arange(length, dtype=jnp.float32) / length
    source = CB_ONE * omega * cells[5] - CW_ONE * cells[5] * eddy / (distance * distance)
    residual = balance / volume
    return jnp.concatenate([residual[0:5], (residual[5] - source)[None]], 0)


def time_limit(cells, metric):
    geometry = metric.astype(jnp.float32)
    total = (
        euler_flux(cells, geometry[0:3])[1]
        + euler_flux(cells, geometry[3:6])[1]
        + euler_flux(cells, geometry[6:9])[1]
    )
    return jnp.min(geometry[9] / total)


def face_layers(cells):
    return jnp.stack([cells[:, 0], cells[:, -1], cells[:, :, 0], cells[:, :, -1]], 0)


def boundary_halo(fetched, own, flip, bc_code):
    turned = jnp.where(flip[..., None, None, None] == 1, jnp.flip(fetched, -2), fetched)
    wall = own * wall_sign()[:, None, None]
    freely = jnp.broadcast_to(free_stream()[:, None, None], own.shape)
    code = bc_code[..., None, None, None]
    return jnp.where(
        code == 0, turned, jnp.where(code == 1, wall, jnp.where(code == 2, freely, own))
    )


def slot_of(marked, keys):
    same = marked[:, None] & marked[None, :]
    return jnp.sum(same & (keys[None, :] < keys[:, None]), axis=1)


def per_device(state, metrics, nbr_block, nbr_face, flip, bc_code):
    blocks = state.shape[0]
    groups = lax.axis_size("gy")
    grid_col = lax.axis_index("gy")
    grid_row = lax.axis_index("gx")
    partner = nbr_block.reshape(-1)
    facing = nbr_face.reshape(-1)
    interface = bc_code.reshape(-1) == 0
    far_device = partner // blocks
    far_row = far_device // groups
    far_col = far_device % groups
    own_key = jnp.arange(partner.shape[0], dtype=jnp.int32)
    far_key = partner % blocks * 4 + facing

    def toward(step_row, step_col):
        return interface & (far_row == grid_row + step_row) & (far_col == grid_col + step_col)

    def plan(step_row, step_col):
        sending = toward(step_row, step_col)
        taking = toward(-step_row, -step_col)
        return (sending, slot_of(sending, own_key), taking, slot_of(taking, far_key))

    row_plans = [plan(1, 0), plan(-1, 0)]
    col_plans = [plan(0, 1), plan(0, -1)]

    def pack(flat, sending, send_slot, capacity):
        outgoing = jnp.zeros((capacity,) + flat.shape[1:], jnp.float32)
        return outgoing.at[jnp.where(sending, send_slot, capacity)].set(flat, mode="drop")

    def halos_for(cells):
        layers = jax.vmap(face_layers)(cells)
        flat = layers.reshape((blocks * 4,) + layers.shape[2:])
        fetched = flat[far_key]
        for offset, entry in zip((1, -1), row_plans):
            outgoing = pack(flat, entry[0], entry[1], 1)
            incoming = shifted(outgoing, "gx", offset)
            fetched = jnp.where(
                entry[2][:, None, None, None], incoming[jnp.minimum(entry[3], 0)], fetched
            )
        for offset, entry in zip((1, -1), col_plans):
            outgoing = pack(flat, entry[0], entry[1], blocks)
            incoming = shifted(outgoing, "gy", offset)
            fetched = jnp.where(
                entry[2][:, None, None, None], incoming[jnp.minimum(entry[3], blocks - 1)], fetched
            )
        fetched = fetched.reshape(layers.shape)
        return boundary_halo(fetched, layers, flip, bc_code)

    def residual_local(cells):
        halos = halos_for(cells)
        return lax.map(
            lambda operands: block_residual(operands[0], operands[1], operands[2]),
            (cells, halos, metrics),
            batch_size=2,
        )

    limits = jax.vmap(time_limit)(state, metrics)
    gathered = lax.all_gather(jnp.broadcast_to(jnp.min(limits), (1024,)), ("gx", "gy"), tiled=True)
    step = CFL_NUMBER * jnp.min(gathered)
    first = residual_local(state)
    middle = state - 0.5 * step * first
    second = residual_local(middle)
    return (state - step * second, second)


def solution(mesh):
    return jax.shard_map(
        per_device,
        mesh=mesh,
        in_specs=(
            P(("gx", "gy"), None, None, None, None),
            P(("gx", "gy"), None, None, None, None),
            P(("gx", "gy"), None),
            P(("gx", "gy"), None),
            P(("gx", "gy"), None),
            P(("gx", "gy"), None),
        ),
        out_specs=(
            P(("gx", "gy"), None, None, None, None),
            P(("gx", "gy"), None, None, None, None),
        ),
        check_vma=False,
    )
```

```python
import jax
import jax.numpy as jnp
from jax import lax
from jax.sharding import PartitionSpec as P

GAMMA = 1.4
GAMMA_MINUS = 0.4
VISCOSITY = 0.02
CFL_NUMBER = 0.5
CB_ONE = 0.1355
CW_ONE = 3.24


def shifted(value, axis, steps):
    count = lax.axis_size(axis)
    initial, last = (max(0, -steps), min(count, count - steps))
    return lax.ppermute(value, axis, [(source, source + steps) for source in range(initial, last)])


def wall_sign():
    return jnp.array([1.0, -1.0, -1.0, -1.0, 1.0, -1.0], jnp.float32)


def free_stream():
    return jnp.array([1.0, 0.5, 0.0, 0.1, 2.1325, 0.05], jnp.float32)


def euler_flux(cons, area):
    density = cons[0]
    velocity = cons[1:4] / density
    pressure = GAMMA_MINUS * (cons[4] - 0.5 * jnp.sum(cons[1:4] * velocity, axis=0))
    normal = jnp.sum(velocity * area, axis=0)
    sound = jnp.sqrt(GAMMA * jnp.abs(pressure) / density)
    flux = jnp.concatenate(
        [
            cons[0:1] * normal,
            cons[1:4] * normal + pressure * area,
            ((cons[4] + pressure) * normal)[None],
            (cons[5] * normal)[None],
        ],
        0,
    )
    speed = jnp.abs(normal) + sound * jnp.sqrt(jnp.sum(area * area, axis=0))
    return (flux, speed)


def face_average(values, axis):
    count = values.shape[axis]
    padded = jnp.concatenate(
        [
            lax.slice_in_dim(values, 0, 1, axis=axis),
            values,
            lax.slice_in_dim(values, count - 1, count, axis=axis),
        ],
        axis,
    )
    return 0.5 * (
        lax.slice_in_dim(padded, 0, count + 1, axis=axis)
        + lax.slice_in_dim(padded, 1, count + 2, axis=axis)
    )


def flux_balance(padded, normals, volume, axis):
    count = normals.shape[axis]
    area = face_average(normals, axis)
    face_volume = face_average(volume, axis - 1)
    left = lax.slice_in_dim(padded, 0, count + 1, axis=axis)
    right = lax.slice_in_dim(padded, 1, count + 2, axis=axis)
    flux_left, speed_left = euler_flux(left, area)
    flux_right, speed_right = euler_flux(right, area)
    jump = right - left
    flux = 0.5 * (flux_left + flux_right) - 0.5 * jnp.maximum(speed_left, speed_right) * jump
    eddy = 0.5 * (left[5] / left[0] + right[5] / right[0])
    coeff = (VISCOSITY + eddy) * jnp.sum(area * area, axis=0) / face_volume
    viscous = jnp.concatenate([jnp.zeros_like(jump[0:1]), coeff * jump[1:]], 0)
    flux = flux - viscous
    return lax.slice_in_dim(flux, 1, count + 1, axis=axis) - lax.slice_in_dim(
        flux, 0, count, axis=axis
    )


def velocity_change(padded, axis):
    count = padded.shape[axis] - 2
    velocity = padded[1:4] / padded[0]
    return 0.5 * (
        lax.slice_in_dim(velocity, 2, count + 2, axis=axis)
        - lax.slice_in_dim(velocity, 0, count, axis=axis)
    )


def block_residual(cells, halos, metric):
    length = cells.shape[3]
    geometry = metric.astype(jnp.float32)
    normal_i, normal_j, normal_k, volume = (
        geometry[0:3],
        geometry[3:6],
        geometry[6:9],
        geometry[9],
    )
    along_i = jnp.concatenate([halos[0][:, None], cells, halos[1][:, None]], 1)
    along_j = jnp.concatenate([halos[2][:, :, None], cells, halos[3][:, :, None]], 2)
    wall = cells[:, :, :, 0:1] * wall_sign()[:, None, None, None]
    freely = jnp.broadcast_to(free_stream()[:, None, None, None], wall.shape)
    along_k = jnp.concatenate([wall, cells, freely], 3)
    balance = (
        flux_balance(along_i, normal_i, volume, 1)
        + flux_balance(along_j, normal_j, volume, 2)
        + flux_balance(along_k, normal_k, volume, 3)
    )
    tensor = (
        velocity_change(along_i, 1)[:, None] * normal_i[None]
        + velocity_change(along_j, 2)[:, None] * normal_j[None]
        + velocity_change(along_k, 3)[:, None] * normal_k[None]
    ) / volume
    vorticity = jnp.stack(
        [tensor[2, 1] - tensor[1, 2], tensor[0, 2] - tensor[2, 0], tensor[1, 0] - tensor[0, 1]], 0
    )
    omega = jnp.sqrt(jnp.sum(vorticity * vorticity, axis=0) + 0.0001)
    eddy = cells[5] / cells[0]
    distance = 1.0 + 4.0 * jnp.arange(length, dtype=jnp.float32) / length
    source = CB_ONE * omega * cells[5] - CW_ONE * cells[5] * eddy / (distance * distance)
    residual = balance / volume
    return jnp.concatenate([residual[0:5], (residual[5] - source)[None]], 0)


def time_limit(cells, metric):
    geometry = metric.astype(jnp.float32)
    total = (
        euler_flux(cells, geometry[0:3])[1]
        + euler_flux(cells, geometry[3:6])[1]
        + euler_flux(cells, geometry[6:9])[1]
    )
    return jnp.min(geometry[9] / total)


def face_layers(cells):
    return jnp.stack([cells[:, 0], cells[:, -1], cells[:, :, 0], cells[:, :, -1]], 0)


def boundary_halo(fetched, own, flip, bc_code):
    turned = jnp.where(flip[..., None, None, None] == 1, jnp.flip(fetched, -2), fetched)
    wall = own * wall_sign()[:, None, None]
    freely = jnp.broadcast_to(free_stream()[:, None, None], own.shape)
    code = bc_code[..., None, None, None]
    return jnp.where(
        code == 0, turned, jnp.where(code == 1, wall, jnp.where(code == 2, freely, own))
    )


def slot_of(marked, keys):
    same = marked[:, None] & marked[None, :]
    return jnp.sum(same & (keys[None, :] < keys[:, None]), axis=1)


def per_device(state, metrics, nbr_block, nbr_face, flip, bc_code):
    blocks = state.shape[0]
    groups = lax.axis_size("gy")
    grid_col = lax.axis_index("gy")
    grid_row = lax.axis_index("gx")
    partner = nbr_block.reshape(-1)
    facing = nbr_face.reshape(-1)
    interface = bc_code.reshape(-1) == 0
    far_device = partner // blocks
    far_row = far_device // groups
    far_col = far_device % groups
    own_key = jnp.arange(partner.shape[0], dtype=jnp.int32)
    far_key = partner % blocks * 4 + facing

    def toward(step_row, step_col):
        return interface & (far_row == grid_row + step_row) & (far_col == grid_col + step_col)

    def plan(step_row, step_col):
        sending = toward(step_row, step_col)
        taking = toward(-step_row, -step_col)
        return (sending, slot_of(sending, own_key), taking, slot_of(taking, far_key))

    row_plans = [plan(1, 0), plan(-1, 0)]
    col_plans = [plan(0, 1), plan(0, -1)]

    def pack(flat, sending, send_slot, capacity):
        outgoing = jnp.zeros((capacity,) + flat.shape[1:], jnp.float32)
        return outgoing.at[jnp.where(sending, send_slot, capacity)].set(flat, mode="drop")

    def halos_for(cells):
        layers = jax.vmap(face_layers)(cells)
        flat = layers.reshape((blocks * 4,) + layers.shape[2:])
        fetched = flat[far_key]
        for offset, entry in zip((1, -1), row_plans):
            outgoing = pack(flat, entry[0], entry[1], 1)
            incoming = shifted(outgoing, "gx", offset)
            fetched = jnp.where(
                entry[2][:, None, None, None], incoming[jnp.minimum(entry[3], 0)], fetched
            )
        for offset, entry in zip((1, -1), col_plans):
            outgoing = pack(flat, entry[0], entry[1], blocks)
            incoming = shifted(outgoing, "gy", offset)
            fetched = jnp.where(
                entry[2][:, None, None, None], incoming[jnp.minimum(entry[3], blocks - 1)], fetched
            )
        return fetched.reshape(layers.shape), layers

    def residual_local(cells, fetched, layers):
        halos = boundary_halo(fetched, layers, flip, bc_code)
        return lax.map(
            lambda operands: block_residual(operands[0], operands[1], operands[2]),
            (cells, halos, metrics),
        )

    limits = jax.vmap(time_limit)(state, metrics)
    gathered = lax.all_gather(jnp.broadcast_to(jnp.min(limits), (1024,)), ("gx", "gy"), tiled=True)
    fetched_state, layers_state = halos_for(state)
    first = residual_local(state, fetched_state, layers_state)
    fetched_first, _ = halos_for(first)
    gathered, fetched_first = lax.optimization_barrier((gathered, fetched_first))
    step = CFL_NUMBER * jnp.min(gathered)
    scale = 0.5 * step
    middle = state - scale * first
    fetched_middle = fetched_state - scale * fetched_first
    second = residual_local(middle, fetched_middle, jax.vmap(face_layers)(middle))
    return (state - step * second, second)


def solution(mesh):
    return jax.shard_map(
        per_device,
        mesh=mesh,
        in_specs=(
            P(("gx", "gy"), None, None, None, None),
            P(("gx", "gy"), None, None, None, None),
            P(("gx", "gy"), None),
            P(("gx", "gy"), None),
            P(("gx", "gy"), None),
            P(("gx", "gy"), None),
        ),
        out_specs=(
            P(("gx", "gy"), None, None, None, None),
            P(("gx", "gy"), None, None, None, None),
        ),
        check_vma=False,
    )
```

```python
import jax
import jax.numpy as jnp
from jax import lax
from jax.sharding import PartitionSpec as P

GAMMA = 1.4
GAMMA_MINUS = 0.4
VISCOSITY = 0.02
CFL_NUMBER = 0.5
CB_ONE = 0.1355
CW_ONE = 3.24


def shifted(value, axis, steps):
    count = lax.axis_size(axis)
    initial, last = (max(0, -steps), min(count, count - steps))
    return lax.ppermute(value, axis, [(source, source + steps) for source in range(initial, last)])


def wall_sign():
    return jnp.array([1.0, -1.0, -1.0, -1.0, 1.0, -1.0], jnp.float32)


def free_stream():
    return jnp.array([1.0, 0.5, 0.0, 0.1, 2.1325, 0.05], jnp.float32)


def euler_flux(cons, area):
    density = cons[0]
    velocity = cons[1:4] / density
    pressure = GAMMA_MINUS * (cons[4] - 0.5 * jnp.sum(cons[1:4] * velocity, axis=0))
    normal = jnp.sum(velocity * area, axis=0)
    sound = jnp.sqrt(GAMMA * jnp.abs(pressure) / density)
    flux = jnp.concatenate(
        [
            cons[0:1] * normal,
            cons[1:4] * normal + pressure * area,
            ((cons[4] + pressure) * normal)[None],
            (cons[5] * normal)[None],
        ],
        0,
    )
    speed = jnp.abs(normal) + sound * jnp.sqrt(jnp.sum(area * area, axis=0))
    return (flux, speed)


def face_average(values, axis):
    count = values.shape[axis]
    padded = jnp.concatenate(
        [
            lax.slice_in_dim(values, 0, 1, axis=axis),
            values,
            lax.slice_in_dim(values, count - 1, count, axis=axis),
        ],
        axis,
    )
    return 0.5 * (
        lax.slice_in_dim(padded, 0, count + 1, axis=axis)
        + lax.slice_in_dim(padded, 1, count + 2, axis=axis)
    )


def flux_balance(padded, normals, volume, axis):
    count = normals.shape[axis]
    area = face_average(normals, axis)
    face_volume = face_average(volume, axis - 1)
    left = lax.slice_in_dim(padded, 0, count + 1, axis=axis)
    right = lax.slice_in_dim(padded, 1, count + 2, axis=axis)
    flux_left, speed_left = euler_flux(left, area)
    flux_right, speed_right = euler_flux(right, area)
    jump = right - left
    flux = 0.5 * (flux_left + flux_right) - 0.5 * jnp.maximum(speed_left, speed_right) * jump
    eddy = 0.5 * (left[5] / left[0] + right[5] / right[0])
    coeff = (VISCOSITY + eddy) * jnp.sum(area * area, axis=0) / face_volume
    viscous = jnp.concatenate([jnp.zeros_like(jump[0:1]), coeff * jump[1:]], 0)
    flux = flux - viscous
    return lax.slice_in_dim(flux, 1, count + 1, axis=axis) - lax.slice_in_dim(
        flux, 0, count, axis=axis
    )


def velocity_change(padded, axis):
    count = padded.shape[axis] - 2
    velocity = padded[1:4] / padded[0]
    return 0.5 * (
        lax.slice_in_dim(velocity, 2, count + 2, axis=axis)
        - lax.slice_in_dim(velocity, 0, count, axis=axis)
    )


def block_residual(cells, halos, metric):
    length = cells.shape[3]
    geometry = metric.astype(jnp.float32)
    normal_i, normal_j, normal_k, volume = (
        geometry[0:3],
        geometry[3:6],
        geometry[6:9],
        geometry[9],
    )
    along_i = jnp.concatenate([halos[0][:, None], cells, halos[1][:, None]], 1)
    along_j = jnp.concatenate([halos[2][:, :, None], cells, halos[3][:, :, None]], 2)
    wall = cells[:, :, :, 0:1] * wall_sign()[:, None, None, None]
    freely = jnp.broadcast_to(free_stream()[:, None, None, None], wall.shape)
    along_k = jnp.concatenate([wall, cells, freely], 3)
    balance = (
        flux_balance(along_i, normal_i, volume, 1)
        + flux_balance(along_j, normal_j, volume, 2)
        + flux_balance(along_k, normal_k, volume, 3)
    )
    tensor = (
        velocity_change(along_i, 1)[:, None] * normal_i[None]
        + velocity_change(along_j, 2)[:, None] * normal_j[None]
        + velocity_change(along_k, 3)[:, None] * normal_k[None]
    ) / volume
    vorticity = jnp.stack(
        [tensor[2, 1] - tensor[1, 2], tensor[0, 2] - tensor[2, 0], tensor[1, 0] - tensor[0, 1]], 0
    )
    omega = jnp.sqrt(jnp.sum(vorticity * vorticity, axis=0) + 0.0001)
    eddy = cells[5] / cells[0]
    distance = 1.0 + 4.0 * jnp.arange(length, dtype=jnp.float32) / length
    source = CB_ONE * omega * cells[5] - CW_ONE * cells[5] * eddy / (distance * distance)
    residual = balance / volume
    return jnp.concatenate([residual[0:5], (residual[5] - source)[None]], 0)


def time_limit(cells, metric):
    geometry = metric.astype(jnp.float32)
    total = (
        euler_flux(cells, geometry[0:3])[1]
        + euler_flux(cells, geometry[3:6])[1]
        + euler_flux(cells, geometry[6:9])[1]
    )
    return jnp.min(geometry[9] / total)


def face_layers(cells):
    return jnp.stack([cells[:, 0], cells[:, -1], cells[:, :, 0], cells[:, :, -1]], 0)


def boundary_halo(fetched, own, flip, bc_code):
    turned = jnp.where(flip[..., None, None, None] == 1, jnp.flip(fetched, -2), fetched)
    wall = own * wall_sign()[:, None, None]
    freely = jnp.broadcast_to(free_stream()[:, None, None], own.shape)
    code = bc_code[..., None, None, None]
    return jnp.where(
        code == 0, turned, jnp.where(code == 1, wall, jnp.where(code == 2, freely, own))
    )


def slot_of(marked, keys):
    same = marked[:, None] & marked[None, :]
    return jnp.sum(same & (keys[None, :] < keys[:, None]), axis=1)


def per_device(state, metrics, nbr_block, nbr_face, flip, bc_code):
    blocks = state.shape[0]
    groups = lax.axis_size("gy")
    grid_col = lax.axis_index("gy")
    grid_row = lax.axis_index("gx")
    partner = nbr_block.reshape(-1)
    facing = nbr_face.reshape(-1)
    interface = bc_code.reshape(-1) == 0
    far_device = partner // blocks
    far_row = far_device // groups
    far_col = far_device % groups
    own_key = jnp.arange(partner.shape[0], dtype=jnp.int32)
    far_key = partner % blocks * 4 + facing

    def toward(step_row, step_col):
        return interface & (far_row == grid_row + step_row) & (far_col == grid_col + step_col)

    def plan(step_row, step_col):
        sending = toward(step_row, step_col)
        taking = toward(-step_row, -step_col)
        return (sending, slot_of(sending, own_key), taking, slot_of(taking, far_key))

    row_plans = [plan(1, 0), plan(-1, 0)]
    col_plans = [plan(0, 1), plan(0, -1)]

    def pack(flat, sending, send_slot, capacity):
        outgoing = jnp.zeros((capacity,) + flat.shape[1:], jnp.float32)
        return outgoing.at[jnp.where(sending, send_slot, capacity)].set(flat, mode="drop")

    def halos_for(cells):
        layers = jax.vmap(face_layers)(cells)
        flat = layers.reshape((blocks * 4,) + layers.shape[2:])
        fetched = flat[far_key]
        for offset, entry in zip((1, -1), row_plans):
            outgoing = pack(flat, entry[0], entry[1], 1)
            incoming = shifted(outgoing, "gx", offset)
            fetched = jnp.where(
                entry[2][:, None, None, None], incoming[jnp.minimum(entry[3], 0)], fetched
            )
        for offset, entry in zip((1, -1), col_plans):
            outgoing = pack(flat, entry[0], entry[1], blocks)
            incoming = shifted(outgoing, "gy", offset)
            fetched = jnp.where(
                entry[2][:, None, None, None], incoming[jnp.minimum(entry[3], blocks - 1)], fetched
            )
        return fetched.reshape(layers.shape), layers

    def residual_local(cells, fetched, layers):
        halos = boundary_halo(fetched, layers, flip, bc_code)
        return lax.map(
            lambda operands: block_residual(operands[0], operands[1], operands[2]),
            (cells, halos, metrics),
        )

    limits = jax.vmap(time_limit)(state, metrics)
    gathered = lax.all_gather(jnp.broadcast_to(jnp.min(limits), (1024,)), ("gx", "gy"), tiled=True)
    fetched_state, layers_state = halos_for(state)
    first = residual_local(state, fetched_state, layers_state)
    fetched_first, _ = halos_for(first)
    gathered, fetched_first = lax.optimization_barrier((gathered, fetched_first))
    step = CFL_NUMBER * jnp.min(gathered[:: gathered.shape[0] // (lax.axis_size("gx") * lax.axis_size("gy"))])
    scale = 0.5 * step
    middle = state - scale * first
    fetched_middle = fetched_state - scale * fetched_first
    second = residual_local(middle, fetched_middle, jax.vmap(face_layers)(middle))
    return (state - step * second, second)


def solution(mesh):
    return jax.shard_map(
        per_device,
        mesh=mesh,
        in_specs=(
            P(("gx", "gy"), None, None, None, None),
            P(("gx", "gy"), None, None, None, None),
            P(("gx", "gy"), None),
            P(("gx", "gy"), None),
            P(("gx", "gy"), None),
            P(("gx", "gy"), None),
        ),
        out_specs=(
            P(("gx", "gy"), None, None, None, None),
            P(("gx", "gy"), None, None, None, None),
        ),
        check_vma=False,
    )
```

```python
import jax
import jax.numpy as jnp
from jax import lax
from jax.sharding import PartitionSpec as P

GAMMA = 1.4
GAMMA_MINUS = 0.4
VISCOSITY = 0.02
CFL_NUMBER = 0.5
CB_ONE = 0.1355
CW_ONE = 3.24


def shifted(value, axis, steps):
    count = lax.axis_size(axis)
    initial, last = (max(0, -steps), min(count, count - steps))
    return lax.ppermute(value, axis, [(source, source + steps) for source in range(initial, last)])


def wall_sign():
    return jnp.array([1.0, -1.0, -1.0, -1.0, 1.0, -1.0], jnp.float32)


def free_stream():
    return jnp.array([1.0, 0.5, 0.0, 0.1, 2.1325, 0.05], jnp.float32)


def euler_flux(cons, area):
    density = cons[0]
    velocity = cons[1:4] / density
    pressure = GAMMA_MINUS * (cons[4] - 0.5 * jnp.sum(cons[1:4] * velocity, axis=0))
    normal = jnp.sum(velocity * area, axis=0)
    sound = jnp.sqrt(GAMMA * jnp.abs(pressure) / density)
    flux = jnp.concatenate(
        [
            cons[0:1] * normal,
            cons[1:4] * normal + pressure * area,
            ((cons[4] + pressure) * normal)[None],
            (cons[5] * normal)[None],
        ],
        0,
    )
    speed = jnp.abs(normal) + sound * jnp.sqrt(jnp.sum(area * area, axis=0))
    return (flux, speed)


def face_average(values, axis):
    count = values.shape[axis]
    padded = jnp.concatenate(
        [
            lax.slice_in_dim(values, 0, 1, axis=axis),
            values,
            lax.slice_in_dim(values, count - 1, count, axis=axis),
        ],
        axis,
    )
    return 0.5 * (
        lax.slice_in_dim(padded, 0, count + 1, axis=axis)
        + lax.slice_in_dim(padded, 1, count + 2, axis=axis)
    )


def flux_balance(padded, normals, volume, axis):
    count = normals.shape[axis]
    area = face_average(normals, axis)
    face_volume = face_average(volume, axis - 1)
    left = lax.slice_in_dim(padded, 0, count + 1, axis=axis)
    right = lax.slice_in_dim(padded, 1, count + 2, axis=axis)
    flux_left, speed_left = euler_flux(left, area)
    flux_right, speed_right = euler_flux(right, area)
    jump = right - left
    flux = 0.5 * (flux_left + flux_right) - 0.5 * jnp.maximum(speed_left, speed_right) * jump
    eddy = 0.5 * (left[5] / left[0] + right[5] / right[0])
    coeff = (VISCOSITY + eddy) * jnp.sum(area * area, axis=0) / face_volume
    viscous = jnp.concatenate([jnp.zeros_like(jump[0:1]), coeff * jump[1:]], 0)
    flux = flux - viscous
    return lax.slice_in_dim(flux, 1, count + 1, axis=axis) - lax.slice_in_dim(
        flux, 0, count, axis=axis
    )


def velocity_change(padded, axis):
    count = padded.shape[axis] - 2
    velocity = padded[1:4] / padded[0]
    return 0.5 * (
        lax.slice_in_dim(velocity, 2, count + 2, axis=axis)
        - lax.slice_in_dim(velocity, 0, count, axis=axis)
    )


def block_residual(cells, halos, metric):
    length = cells.shape[3]
    geometry = metric.astype(jnp.float32)
    normal_i, normal_j, normal_k, volume = (
        geometry[0:3],
        geometry[3:6],
        geometry[6:9],
        geometry[9],
    )
    along_i = jnp.concatenate([halos[0][:, None], cells, halos[1][:, None]], 1)
    along_j = jnp.concatenate([halos[2][:, :, None], cells, halos[3][:, :, None]], 2)
    wall = cells[:, :, :, 0:1] * wall_sign()[:, None, None, None]
    freely = jnp.broadcast_to(free_stream()[:, None, None, None], wall.shape)
    along_k = jnp.concatenate([wall, cells, freely], 3)
    balance = (
        flux_balance(along_i, normal_i, volume, 1)
        + flux_balance(along_j, normal_j, volume, 2)
        + flux_balance(along_k, normal_k, volume, 3)
    )
    tensor = (
        velocity_change(along_i, 1)[:, None] * normal_i[None]
        + velocity_change(along_j, 2)[:, None] * normal_j[None]
        + velocity_change(along_k, 3)[:, None] * normal_k[None]
    ) / volume
    vorticity = jnp.stack(
        [tensor[2, 1] - tensor[1, 2], tensor[0, 2] - tensor[2, 0], tensor[1, 0] - tensor[0, 1]], 0
    )
    omega = jnp.sqrt(jnp.sum(vorticity * vorticity, axis=0) + 0.0001)
    eddy = cells[5] / cells[0]
    distance = 1.0 + 4.0 * jnp.arange(length, dtype=jnp.float32) / length
    source = CB_ONE * omega * cells[5] - CW_ONE * cells[5] * eddy / (distance * distance)
    residual = balance / volume
    return jnp.concatenate([residual[0:5], (residual[5] - source)[None]], 0)


def time_limit(cells, metric):
    geometry = metric.astype(jnp.float32)
    total = (
        euler_flux(cells, geometry[0:3])[1]
        + euler_flux(cells, geometry[3:6])[1]
        + euler_flux(cells, geometry[6:9])[1]
    )
    return jnp.min(geometry[9] / total)


def face_layers(cells):
    return jnp.stack([cells[:, 0], cells[:, -1], cells[:, :, 0], cells[:, :, -1]], 0)


def boundary_halo(fetched, own, flip, bc_code):
    turned = jnp.where(flip[..., None, None, None] == 1, jnp.flip(fetched, -2), fetched)
    wall = own * wall_sign()[:, None, None]
    freely = jnp.broadcast_to(free_stream()[:, None, None], own.shape)
    code = bc_code[..., None, None, None]
    return jnp.where(
        code == 0, turned, jnp.where(code == 1, wall, jnp.where(code == 2, freely, own))
    )


def slot_of(marked, keys):
    same = marked[:, None] & marked[None, :]
    return jnp.sum(same & (keys[None, :] < keys[:, None]), axis=1)


def per_device(state, metrics, nbr_block, nbr_face, flip, bc_code):
    blocks = state.shape[0]
    groups = lax.axis_size("gy")
    grid_col = lax.axis_index("gy")
    grid_row = lax.axis_index("gx")
    partner = nbr_block.reshape(-1)
    facing = nbr_face.reshape(-1)
    interface = bc_code.reshape(-1) == 0
    far_device = partner // blocks
    far_row = far_device // groups
    far_col = far_device % groups
    own_key = jnp.arange(partner.shape[0], dtype=jnp.int32)
    far_key = partner % blocks * 4 + facing

    def toward(step_row, step_col):
        return interface & (far_row == grid_row + step_row) & (far_col == grid_col + step_col)

    def plan(step_row, step_col):
        sending = toward(step_row, step_col)
        taking = toward(-step_row, -step_col)
        return (sending, slot_of(sending, own_key), taking, slot_of(taking, far_key))

    row_plans = [plan(1, 0), plan(-1, 0)]
    col_plans = [plan(0, 1), plan(0, -1)]

    def pack(flat, sending, send_slot, capacity):
        outgoing = jnp.zeros((capacity,) + flat.shape[1:], jnp.float32)
        return outgoing.at[jnp.where(sending, send_slot, capacity)].set(flat, mode="drop")

    def halos_for(cells):
        layers = jax.vmap(face_layers)(cells)
        flat = layers.reshape((blocks * 4,) + layers.shape[2:])
        fetched = flat[far_key]
        for offset, entry in zip((1, -1), row_plans):
            outgoing = pack(flat, entry[0], entry[1], 1)
            incoming = shifted(outgoing, "gx", offset)
            fetched = jnp.where(
                entry[2][:, None, None, None], incoming[jnp.minimum(entry[3], 0)], fetched
            )
        for offset, entry in zip((1, -1), col_plans):
            outgoing = pack(flat, entry[0], entry[1], blocks)
            incoming = shifted(outgoing, "gy", offset)
            fetched = jnp.where(
                entry[2][:, None, None, None], incoming[jnp.minimum(entry[3], blocks - 1)], fetched
            )
        return fetched.reshape(layers.shape), layers

    def residual_local(cells, fetched, layers):
        halos = boundary_halo(fetched, layers, flip, bc_code)
        return lax.map(
            lambda operands: block_residual(operands[0], operands[1], operands[2]),
            (cells, halos, metrics),
        )

    def residual_into(buffer, cells, fetched, layers):
        halos = boundary_halo(fetched, layers, flip, bc_code)

        def body(index, out):
            return out.at[index].set(block_residual(cells[index], halos[index], metrics[index]))

        return lax.fori_loop(0, blocks, body, buffer)

    limits = jax.vmap(time_limit)(state, metrics)
    gathered = lax.all_gather(jnp.broadcast_to(jnp.min(limits), (1024,)), ("gx", "gy"), tiled=True)
    fetched_state, layers_state = halos_for(state)
    first = residual_local(state, fetched_state, layers_state)
    fetched_first, _ = halos_for(first)
    gathered, fetched_first = lax.optimization_barrier((gathered, fetched_first))
    step = CFL_NUMBER * jnp.min(gathered)
    scale = 0.5 * step
    middle = state - scale * first
    fetched_middle = fetched_state - scale * fetched_first
    second = residual_into(first, middle, fetched_middle, jax.vmap(face_layers)(middle))
    return (state - step * second, second)


def solution(mesh):
    return jax.shard_map(
        per_device,
        mesh=mesh,
        in_specs=(
            P(("gx", "gy"), None, None, None, None),
            P(("gx", "gy"), None, None, None, None),
            P(("gx", "gy"), None),
            P(("gx", "gy"), None),
            P(("gx", "gy"), None),
            P(("gx", "gy"), None),
        ),
        out_specs=(
            P(("gx", "gy"), None, None, None, None),
            P(("gx", "gy"), None, None, None, None),
        ),
        check_vma=False,
    )
```
